256 devices in a mesh: row: 4 (over x), col: 4 (over z_lo), leaf: 16 (over z_hi, y, core).
Axes of the slice: x: 4, y: 4, z: 8 (z_hi: 2, z_lo: 4; z = z_hi * 4 + z_lo), core: 2. Of those that a mesh axis runs over, the one named last changes fastest.
Arguments:
- copies: float32 [16, 3072, 3072], P('leaf', 'row', 'col'), may hold values from -4 to 4
- left_panels: bfloat16 [4, 2, 16, 3072, 1024], P(None, None, 'leaf', 'row', 'col'), may hold values from -6 to 6
- upper_panels: bfloat16 [4, 2, 16, 1024, 3072], P(None, None, 'leaf', 'row', 'col'), may hold values from -0.09375 to 0.09375
- live_blocks: int32 [4, 2, 16, 12], P(None, None, 'leaf'), may hold values from 0 to 23, as said below
Outputs:
- fronts: float32 [16, 3072, 3072], P('leaf', 'row', 'col')
The draws below stay inside these ranges and needn't reach their ends.
Inputs may be any that keep to these rules, and one draw needn't show every extreme that they name: For each level l, node n and layer p, entries s * 3 to (s + 1) * 3 - 1 of live_blocks[l, n, p] are 3 distinct block numbers of slab s, that is, of s * 6 to (s + 1) * 6 - 1, in any order, for s from 0 to 3.
All inputs are finite; a program needn't handle non-finite values.
Results may differ from the reference program's by a relative error of at most 0.0003.
Values may be sent and summed in bfloat16 or wider, within the bound.
No kernel may reach another device: no remote copies, remote signals or barrier semaphores. Data moves between devices by JAX's collectives and lax.ppermute only.
A program may use at most 128 MiB of HBM per device.

```python
import jax
import jax.numpy as jnp

A = 3072
K = 1024
BLK = 128
NODES = 2
LEVELS = 4
LAYERS = 16
SLABS = 4
SLAB_BLOCKS = 6
HALF_BLOCKS = 3
N_LEAF = 16


def draw_live_blocks(key, part):
    draw_count = LEVELS * NODES * LAYERS * SLABS
    subkeys = jax.random.split(jax.random.fold_in(key, 7), draw_count)

    def pick_half(subkey):
        return jax.random.permutation(subkey, SLAB_BLOCKS)[:HALF_BLOCKS].astype(jnp.int32)
    chosen = jax.vmap(pick_half)(subkeys).reshape(LEVELS, NODES, LAYERS, SLABS, HALF_BLOCKS)
    offset = jnp.arange(SLABS, dtype=jnp.int32)[:, None] * SLAB_BLOCKS
    return (chosen + offset).reshape(LEVELS, NODES, LAYERS, SLABS * HALF_BLOCKS)


def block_scale(stream_key, dims, pieces, least, top_value):
    def one(dim, shards_of):
        heights = jax.random.uniform(jax.random.fold_in(jax.random.fold_in(stream_key, 6), dim), (shards_of,), jnp.float32, least / len(pieces), top_value / len(pieces))
        return jnp.repeat(jnp.exp(heights), dims[dim] // shards_of).reshape((-1,) + (1,) * (len(dims) - dim - 1))

    level = one(*pieces[0])
    for cut in pieces[1:]:
        level = level * one(*cut)
    return level


def noise(rng, dims, scale, reach, cuts=(), kind=jnp.bfloat16):
    values = jax.random.normal(rng, dims, jnp.float32) * scale
    if len(cuts) > 0:
        values = block_scale(rng, dims, cuts, -0.22, 0.18) * values
    return jnp.clip(values, min=-reach, max=reach).astype(kind)


def setup_inputs(seed: int = 0) -> dict:
    seeds = jax.random.split(jax.random.key(seed), 5)
    copies = noise(seeds[0], (LAYERS, A, A), 0.3, 4.0, ((0, 16), (1, 4), (2, 4)), jnp.float32)
    left_panels = noise(seeds[1], (LEVELS, NODES, LAYERS, A, K), 1.0, 6.0, ((2, 16), (3, 4), (4, 4)))
    upper_panels = noise(seeds[2], (LEVELS, NODES, LAYERS, K, A), (4 * K) ** -0.5, 0.09375, ((2, 16), (3, 4), (4, 4)))
    live_blocks = draw_live_blocks(jax.random.fold_in(seeds[4], 71), 0)
    return dict(copies=copies, left_panels=left_panels, upper_panels=upper_panels, live_blocks=live_blocks)


def block_rows(block_ids):
    offsets = jnp.arange(BLK, dtype=jnp.int32)
    return (block_ids.astype(jnp.int32)[:, None] * BLK + offsets[None, :]).reshape(-1)


def reference(copies, left_panels, upper_panels, live_blocks):
    current = [copies[layer_id] for layer_id in range(N_LEAF)]
    for height in range(LEVELS):
        stride = 2 ** height
        for layer_id in range(0, N_LEAF, stride):
            change = jnp.zeros((A, A), jnp.float32)
            for node_no in range(NODES):
                rows_used = block_rows(live_blocks[height, node_no, layer_id])
                product = jnp.dot(left_panels[height, node_no, layer_id][rows_used], upper_panels[height, node_no, layer_id][:, rows_used], preferred_element_type=jnp.float32)
                change = change.at[rows_used[:, None], rows_used[None, :]].add(product)
            current[layer_id] = current[layer_id] - change
        if stride < N_LEAF:
            for layer_id in range(0, N_LEAF, 2 * stride):
                summed = current[layer_id] + current[layer_id + stride]
                current[layer_id] = summed
                current[layer_id + stride] = summed
    return jnp.stack(current)
```

```python
import functools

import jax
import jax.numpy as jnp
from jax import lax
from jax.experimental import pallas as pl
from jax.experimental.pallas import tpu as pltpu
from jax.sharding import PartitionSpec as P


AXES = ("row", "col", "leaf")
SIDE = 4
LEAF = 16
BLK = 128
LIVE = 3
SLAB = 6
NODES = 2
KC = 256
BF = jnp.bfloat16
F32 = jnp.float32
ANY = pl.BlockSpec(memory_space=pl.ANY)
VMEM = pl.BlockSpec(memory_space=pltpu.VMEM)
HBM = pl.BlockSpec(memory_space=pltpu.HBM)
SMEM = pl.BlockSpec(memory_space=pltpu.SMEM)

R2 = NODES * 2 * LIVE * 64
R3 = NODES * 2 * LIVE * 32
RU = NODES * LIVE * KC


def send(x, move):
    pairs = []
    for r in range(SIDE):
        for c in range(SIDE):
            for p in range(LEAF):
                to = move(r, c, p)
                if to is not None:
                    flat = [(a * SIDE + b) * LEAF + d for a, b, d in ((r, c, p), to)]
                    pairs.append(tuple(flat))
    return lax.ppermute(x, AXES, pairs)


def to_leaf(delta, when):
    return lambda r, c, p: (r, c, p + delta) if when(p % 2, p // 2 % 4) else None


def flip_leaf(bit, when=lambda core, y: True):
    return lambda r, c, p: (r, c, p ^ bit) if when(p % 2, p // 2 % 4) else None


def gather(left, upper, every):
    lefts, uppers = [left], [upper]
    for e in (2, 1, 3):
        lefts.append(send(left, lambda r, c, p: (r, c ^ e, p) if every or p % 2 == 0 else None))
        uppers.append(send(upper, lambda r, c, p: (r ^ e, c, p) if every or p % 2 == 0 else None))
    return lefts, uppers


ORDER = (0, 2, 1, 3)


def start_all(copies, sem):
    for src, dst in copies:
        pltpu.make_async_copy(src, dst, sem).start()


def wait_for(ref, sem):
    pltpu.make_async_copy(ref, ref, sem).wait()


def live_block(ids, level, n, slab, i):
    return ids[level, n, slab * LIVE + i] - slab * SLAB


def pack_level(ids, role, left, upper, level, lo, uo, sem):
    copies = []
    for n in range(NODES):
        for i in range(LIVE):
            rb = pl.multiple_of(live_block(ids, level, n, role[0], i) * BLK, BLK)
            cb = pl.multiple_of(live_block(ids, level, n, role[1], i) * BLK, BLK)
            for k in range(2):
                copies.append((
                    left.at[level, n, 0, pl.ds(rb, BLK), pl.ds(k * 128, 128)],
                    lo.at[n, k, pl.ds(i * BLK, BLK)],
                ))
            copies.append((upper.at[level, n, 0, :, pl.ds(cb, BLK)], uo.at[n, i]))
    start_all(copies, sem)


def pack0_kernel(ids, role, left, upper, lo, uo, sems):
    pack_level(ids, role, left, upper, 0, lo, uo, sems.at[0])
    wait_for(lo, sems.at[0])
    wait_for(uo, sems.at[0])


def pack_rows(ids, role, left, level, sub, rows, out, base, sem):
    copies = []
    for n in range(NODES):
        for i in range(LIVE):
            rb = pl.multiple_of(live_block(ids, level, n, role[0], i) * BLK + sub * rows, rows)
            for k in range(2):
                copies.append((
                    left.at[level, n, 0, pl.ds(rb, rows), pl.ds(k * 128, 128)],
                    out.at[pl.ds(base + ((n * 2 + k) * LIVE + i) * rows, rows)],
                ))
    start_all(copies, sem)


def pack_cols(ids, role, upper, level, out, base, sem):
    copies = []
    for n in range(NODES):
        for i in range(LIVE):
            cb = pl.multiple_of(live_block(ids, level, n, role[1], i) * BLK, BLK)
            copies.append((
                upper.at[level, n, 0, :, pl.ds(cb, BLK)],
                out.at[pl.ds(base + (n * LIVE + i) * KC, KC)],
            ))
    start_all(copies, sem)


def pack123_kernel(ids, role, left, upper, lo, uo, own, m1, m2, m3, sems):
    pack_level(ids, role, left, upper, 1, lo, uo, sems.at[0])
    for j, (out, half, quarter) in enumerate(((own, 0, 0), (m1, 1, 2))):
        pack_rows(ids, role, left, 2, half, 64, out, 0, sems.at[1 + j])
        pack_rows(ids, role, left, 3, quarter, 32, out, R2, sems.at[1 + j])
        pack_cols(ids, role, upper, 2, out, R2 + R3, sems.at[1 + j])
        pack_cols(ids, role, upper, 3, out, R2 + R3 + RU, sems.at[1 + j])
    for j, (out, quarter) in enumerate(((m2, 1), (m3, 3))):
        pack_rows(ids, role, left, 3, quarter, 32, out, 0, sems.at[3 + j])
        pack_cols(ids, role, upper, 3, out, R3, sems.at[3 + j])
    wait_for(lo, sems.at[0])
    wait_for(uo, sems.at[0])
    for j, out in enumerate((own, m1, m2, m3)):
        wait_for(out, sems.at[1 + j])


def choose_kernel(role, own, m1, m2, m3, zo, xo, sem):
    y = role[3]

    def take(src, parts):
        for a, dst, b, size in parts:
            pltpu.make_async_copy(src.at[pl.ds(a, size)], dst.at[pl.ds(b, size)], sem).start()

    two = ((0, zo, 0, R2), (R2 + R3, xo, 0, RU))
    three = ((R2, zo, R2, R3), (R2 + R3 + RU, xo, RU, RU))
    three_m = ((0, zo, R2, R3), (R3, xo, RU, RU))
    for odd, src in ((0, own), (1, m1)):
        pl.when(y % 2 == odd)(functools.partial(take, src, two))
    for at, src, parts in ((0, own, three), (1, m1, three), (2, m2, three_m), (3, m3, three_m)):
        pl.when(y == at)(functools.partial(take, src, parts))
    wait_for(zo, sem)
    wait_for(xo, sem)


def load_panels(role, lefts, uppers, rows, l_at, u_at, la, ua, sem):
    copies = []
    for e in range(SIDE):
        lj = pl.multiple_of((role[1] ^ ORDER[e]) * KC, KC)
        uj = pl.multiple_of((role[0] ^ ORDER[e]) * KC, KC)
        for n in range(NODES):
            for k in range(2):
                copies.append((
                    lefts[e].at[pl.ds(l_at + (n * 2 + k) * rows, rows)],
                    la.at[n, :, pl.ds(lj + k * 128, 128)],
                ))
            for i in range(LIVE):
                copies.append((
                    uppers[e].at[pl.ds(u_at + (n * LIVE + i) * KC, KC)],
                    ua.at[n, pl.ds(uj, KC), pl.ds(i * BLK, BLK)],
                ))
    start_all(copies, sem)


def subtract(ids, role, level, sub_rows, la, ua, out):
    for n in range(NODES):
        c = jnp.dot(la[n], ua[n], preferred_element_type=F32)
        for i in range(LIVE):
            rb = pl.multiple_of(live_block(ids, level, n, role[0], i) * sub_rows, sub_rows)
            for j in range(LIVE):
                cb = pl.multiple_of(live_block(ids, level, n, role[1], j) * BLK, BLK)
                at = (pl.ds(rb, sub_rows), pl.ds(cb, BLK))
                out[at] -= c[i * sub_rows : (i + 1) * sub_rows, j * BLK : (j + 1) * BLK]


def update0_kernel(ids, role, front, *refs):
    lefts, uppers, (out, la, ua, sem) = refs[:4], refs[4:8], refs[8:]
    load_panels(role, lefts, uppers, LIVE * BLK, 0, 0, la, ua, sem)
    out[...] = front[...]
    wait_for(la, sem)
    wait_for(ua, sem)
    subtract(ids, role, 0, BLK, la, ua, out)


def update1_kernel(ids, role, mine, theirs, *refs):
    lefts, uppers, (keep, give, la, ua, t, sem) = refs[:4], refs[4:8], refs[8:]
    load_panels(role, lefts, uppers, LIVE * BLK, 0, 0, la, ua, sem)
    t[...] = mine[...] + theirs[...]
    wait_for(la, sem)
    wait_for(ua, sem)
    subtract(ids, role, 1, BLK, la, ua, t)
    split(t, keep, give, 64, role[3] % 2)


def split(t, keep, give, rows, which):
    for b in range(SLAB):
        for out, w in ((keep, which), (give, 1 - which)):
            at = pl.multiple_of(b * 2 * rows + w * rows, rows)
            out[pl.ds(b * rows, rows)] = t[pl.ds(at, rows)]


def update2_kernel(ids, role, mine, theirs, *refs):
    lefts, uppers, (s, keep, give, la, ua, t, sem) = refs[:4], refs[4:8], refs[8:]
    load_panels(role, lefts, uppers, LIVE * 64, 0, 0, la, ua, sem)
    total = mine[...] + theirs[...]
    s[...] = total
    t[...] = total
    wait_for(la, sem)
    wait_for(ua, sem)
    subtract(ids, role, 2, 64, la, ua, t)
    split(t, keep, give, 32, role[3] // 2)


def update3_kernel(ids, role, mine, theirs, *refs):
    lefts, uppers, (s, t, la, ua, sem) = refs[:4], refs[4:8], refs[8:]
    load_panels(role, lefts, uppers, LIVE * 32, R2, RU, la, ua, sem)
    total = mine[...] + theirs[...]
    s[...] = total
    t[...] = total
    wait_for(la, sem)
    wait_for(ua, sem)
    subtract(ids, role, 3, 32, la, ua, t)


def finish_kernel(role, t0, r0, s1, r1, s2, s2_from, t3, r3, f8_from1, f8_from2, f8_from3, s2_from1, s2_from3, out, buf, tail, sems):
    core, y = role[2], role[3]

    def rows(src, q, n, sem):
        for b in range(SLAB):
            pltpu.make_async_copy(src.at[pl.ds(b * n, n)], out.at[pl.ds(b * BLK + q * 32, n)], sem).start()

    def quarters(parts):
        for src, q in parts:
            rows(src, q, 32, sems.at[0])
        wait_for(out, sems.at[0])

    @pl.when(core == 1)
    def _():
        a = pltpu.make_async_copy(t0, out, sems.at[0])
        b = pltpu.make_async_copy(r0, buf, sems.at[1])
        a.start()
        b.start()
        a.wait()
        b.wait()
        out[...] += buf[...]

    @pl.when((core == 0) & (y % 2 == 1))
    def _():
        rows(r1, 0, 64, sems.at[0])
        rows(s1, 2, 64, sems.at[0])
        wait_for(out, sems.at[0])

    @pl.when((core == 0) & (y == 2))
    def _():
        quarters(((s2_from, 0), (s2, 1), (s2_from1, 2), (s2_from3, 3)))

    @pl.when((core == 0) & (y == 0))
    def _():
        n = SLAB * 32
        a = pltpu.make_async_copy(t3, tail.at[0], sems.at[1])
        b = pltpu.make_async_copy(r3, tail.at[1], sems.at[2])
        a.start()
        b.start()
        for src, q in ((f8_from2, 1), (f8_from1, 2), (f8_from3, 3)):
            rows(src, q, 32, sems.at[0])
        a.wait()
        b.wait()
        wait_for(buf.at[pl.ds(0, 3 * n)], sems.at[0])
        for b in range(SLAB):
            at = pl.ds(b * 32, 32)
            out[pl.ds(b * BLK, 32)] = tail[0, at] + tail[1, at]


def grant(mib):
    return pltpu.CompilerParams(vmem_limit_bytes=mib << 20)


def sds(*shape, dtype=BF):
    return jax.ShapeDtypeStruct(shape, dtype)


def update_call(kernel, name, ids, role, fronts, lefts, uppers, rows, outs, temp=None):
    scratch = [pltpu.VMEM((NODES, rows, SIDE * KC), BF), pltpu.VMEM((NODES, SIDE * KC, LIVE * BLK), BF)]
    if temp is not None:
        scratch.append(pltpu.VMEM(temp, F32))
    scratch.append(pltpu.SemaphoreType.DMA)
    return pl.pallas_call(
        kernel,
        out_shape=outs,
        in_specs=[SMEM, SMEM] + [VMEM] * len(fronts) + [ANY] * 8,
        out_specs=jax.tree.map(lambda _: VMEM, outs),
        scratch_shapes=scratch,
        name=name,
        compiler_params=grant(16),
        cost_estimate=pl.CostEstimate(
            flops=2 * NODES * rows * LIVE * BLK * SIDE * KC, bytes_accessed=8 << 20, transcendentals=0
        ),
    )(ids, role, *fronts, *lefts, *uppers)


def on_device(copies, left, upper, live):
    row, col, leaf = (lax.axis_index(a) for a in AXES)
    role = jnp.stack([row, col, leaf % 2, leaf // 2 % 4]).astype(jnp.int32)
    ids = live[:, :, 0, :]
    front = copies[0]
    cols = front.shape[1]
    half, quarter = SLAB * 64, SLAB * 32

    lp0, up0 = pl.pallas_call(
        pack0_kernel,
        out_shape=(sds(NODES, 2, LIVE * BLK, 128), sds(NODES, LIVE, KC, BLK)),
        in_specs=[SMEM, SMEM, HBM, HBM],
        out_specs=(VMEM, VMEM),
        scratch_shapes=[pltpu.SemaphoreType.DMA((1,))],
        name="pack0",
        compiler_params=grant(4),
    )(ids, role, left, upper)
    lp0, up0 = lp0.reshape(-1, 128), up0.reshape(-1, 128)
    left, upper, lp0, up0 = lax.optimization_barrier((left, upper, lp0, up0))
    l0, u0 = gather(lp0, up0, True)

    lp1, up1, own, m1, m2, m3 = pl.pallas_call(
        pack123_kernel,
        out_shape=(
            sds(NODES, 2, LIVE * BLK, 128),
            sds(NODES, LIVE, KC, BLK),
            sds(R2 + R3 + 2 * RU, 128),
            sds(R2 + R3 + 2 * RU, 128),
            sds(R3 + RU, 128),
            sds(R3 + RU, 128),
        ),
        in_specs=[SMEM, SMEM, HBM, HBM],
        out_specs=(VMEM,) * 6,
        scratch_shapes=[pltpu.SemaphoreType.DMA((5,))],
        name="pack123",
        compiler_params=grant(8),
    )(ids, role, left, upper)
    lp1, up1 = lp1.reshape(-1, 128), up1.reshape(-1, 128)
    to1 = to_leaf(2, lambda core, y: core == 0 and y % 2 == 0)
    to2 = to_leaf(4, lambda core, y: core == 0 and y == 0)
    to3 = to_leaf(6, lambda core, y: core == 0 and y == 0)
    m1, m2, m3 = send(m1, to1), send(m2, to2), send(m3, to3)
    i1, i2, i3 = (send(ids, to) for to in (to1, to2, to3))
    y = jnp.where(role[2] == 0, role[3], 0)
    ids2 = jnp.where(y % 2 == 0, ids[2], i1[2])
    ids3 = jnp.where(y == 0, ids[3], jnp.where(y == 1, i1[3], jnp.where(y == 2, i2[3], i3[3])))
    ids = jnp.stack([ids[0], ids[1], ids2, ids3])
    z23, x23 = pl.pallas_call(
        choose_kernel,
        out_shape=(sds(R2 + R3, 128), sds(2 * RU, 128)),
        in_specs=[SMEM] + [ANY] * 4,
        out_specs=(VMEM, VMEM),
        scratch_shapes=[pltpu.SemaphoreType.DMA],
        name="choose",
        compiler_params=grant(4),
    )(role, own, m1, m2, m3)

    l0, u0, lp1, up1, z23, x23 = lax.optimization_barrier((l0, u0, lp1, up1, z23, x23))
    l1, u1 = gather(lp1, up1, False)
    l23, u23 = gather(z23, x23, False)

    whole = sds(*front.shape, dtype=F32)
    t0 = update_call(update0_kernel, "update0", ids, role, [front], l0, u0, LIVE * BLK, whole)
    r0 = send(t0, flip_leaf(1))

    halves = sds(half, cols, dtype=F32)
    keep, give = update_call(
        update1_kernel, "update1", ids, role, [t0, r0], l1, u1, LIVE * BLK, (halves, halves), front.shape
    )
    got = send(give, flip_leaf(2, lambda core, y: core == 0))

    quarters = sds(quarter, cols, dtype=F32)
    s1, keep, give = update_call(
        update2_kernel, "update2", ids, role, [keep, got], l23, u23, LIVE * 64, (halves, quarters, quarters), (half, cols)
    )
    got = send(give, flip_leaf(4, lambda core, y: core == 0))
    s1, got = lax.optimization_barrier((s1, got))
    r1 = send(s1, to_leaf(2, lambda core, y: core == 0 and y % 2 == 0))

    s2, t3 = update_call(
        update3_kernel, "update3", ids, role, [keep, got], l23, u23, LIVE * 32, (quarters, quarters)
    )
    r3 = send(t3, flip_leaf(8, lambda core, y: core == 0))
    s2_from = send(s2, to_leaf(4, lambda core, y: core == 0 and y == 0))
    s2_from1 = send(s2, to_leaf(2, lambda core, y: core == 0 and y == 1))
    s2_from3 = send(s2, to_leaf(-2, lambda core, y: core == 0 and y == 3))

    f8 = t3 + r3
    from1 = send(f8, to_leaf(-2, lambda core, y: core == 0 and y == 1))
    from2 = send(f8, to_leaf(-4, lambda core, y: core == 0 and y == 2))
    from3 = send(f8, to_leaf(-6, lambda core, y: core == 0 and y == 3))

    out = pl.pallas_call(
        finish_kernel,
        out_shape=whole,
        in_specs=[SMEM] + [ANY] * 13,
        out_specs=VMEM,
        scratch_shapes=[
            pltpu.VMEM(front.shape, F32),
            pltpu.VMEM((2, quarter, cols), F32),
            pltpu.SemaphoreType.DMA((3,)),
        ],
        name="finish",
        compiler_params=grant(10),
    )(role, t0, r0, s1, r1, s2, s2_from, t3, r3, from1, from2, from3, s2_from1, s2_from3)
    return out[None]


def solution(mesh):
    in_specs = (
        P("leaf", "row", "col"),
        P(None, None, "leaf", "row", "col"),
        P(None, None, "leaf", "row", "col"),
        P(None, None, "leaf", None),
    )
    out_specs = P("leaf", "row", "col")
    return jax.shard_map(
        on_device, mesh=mesh, in_specs=in_specs, out_specs=out_specs, check_vma=False
    )
```

```python
import functools

import jax
import jax.numpy as jnp
from jax import lax
from jax.experimental import pallas as pl
from jax.experimental.pallas import tpu as pltpu
from jax.sharding import PartitionSpec as P


AXES = ("row", "col", "leaf")
SIDE = 4
LEAF = 16
BLK = 128
LIVE = 3
SLAB = 6
NODES = 2
KC = 256
BF = jnp.bfloat16
F32 = jnp.float32
ORDER = (0, 2, 1, 3)
ANY = pl.BlockSpec(memory_space=pl.ANY)
VMEM = pl.BlockSpec(memory_space=pltpu.VMEM)
HBM = pl.BlockSpec(memory_space=pltpu.HBM)
SMEM = pl.BlockSpec(memory_space=pltpu.SMEM)

L1, L2, L3, U = 2 * LIVE * BLK, 2 * LIVE * 64, 2 * LIVE * 32, LIVE * KC
NUM = 16
AT_L2 = (L1, L1 + L2)
AT_L3 = tuple(L1 + 2 * L2 + j * L3 for j in range(4))
AT_U = tuple(L1 + 2 * L2 + 4 * L3 + j * U for j in range(3))
AT_NUM = AT_U[2] + U
PACK = AT_NUM + NUM


def send(x, move):
    pairs = []
    for r in range(SIDE):
        for c in range(SIDE):
            for p in range(LEAF):
                to = move(r, c, p)
                if to is not None:
                    flat = [(a * SIDE + b) * LEAF + d for a, b, d in ((r, c, p), to)]
                    pairs.append(tuple(flat))
    return lax.ppermute(x, AXES, pairs)


def flip_leaf(bits):
    return lambda r, c, p: (r, c, p ^ bits)


def gather(left, upper):
    lefts, uppers = [left], [upper]
    for e in ORDER[1:]:
        lefts.append(send(left, lambda r, c, p: (r, c ^ e, p)))
        uppers.append(send(upper, lambda r, c, p: (r ^ e, c, p)))
    return lefts, uppers


def start_all(copies, sem):
    for src, dst in copies:
        pltpu.make_async_copy(src, dst, sem).start()


def wait_for(ref, sem):
    pltpu.make_async_copy(ref, ref, sem).wait()


def live_block(ids, level, n, slab, i):
    return ids[level, n, slab * LIVE + i] - slab * SLAB


def pack0_kernel(ids, role, left, upper, lo, uo, sems):
    for n in range(NODES):
        for i in range(LIVE):
            rb = pl.multiple_of(live_block(ids, 0, n, role[0], i) * BLK, BLK)
            cb = pl.multiple_of(live_block(ids, 0, n, role[1], i) * BLK, BLK)
            lefts = [(left.at[0, n, 0, pl.ds(rb, BLK), pl.ds(k * 128, 128)], lo.at[n, k, pl.ds(i * BLK, BLK)]) for k in range(2)]
            start_all(lefts, sems.at[0])
            start_all([(upper.at[0, n, 0, :, pl.ds(cb, BLK)], uo.at[n, i])], sems.at[1])
    wait_for(lo, sems.at[0])
    wait_for(uo, sems.at[1])


def pack123_kernel(ids, role, left, upper, w0, w1, nums, sems):
    lane = lax.broadcasted_iota(jnp.int32, (NUM, 128), 1)
    row = jnp.zeros((NUM, 128), F32)
    for level in (1, 2, 3):
        for n in range(NODES):
            for i in range(SIDE * LIVE):
                at = ((level - 1) * NODES + n) * SIDE * LIVE + i
                row = jnp.where(lane == at, ids[level, n, i].astype(F32), row)
    nums[...] = row.astype(BF)
    for n, out in ((1, w1), (0, w0)):
        copies = []
        for i in range(LIVE):
            for level in (1, 2, 3):
                rb = live_block(ids, level, n, role[0], i) * BLK
                for k in range(2):
                    half = pl.ds(k * 128, 128)

                    def piece(offset, rows, at):
                        src = left.at[level, n, 0, pl.ds(pl.multiple_of(rb + offset, rows), rows), half]
                        copies.append((src, out.at[pl.ds(at, rows)]))

                    if level == 1:
                        piece(0, BLK, (k * LIVE + i) * BLK)
                    for core in range(2):
                        if level == 2:
                            for s1 in range(2):
                                piece(core * 64 + s1 * 32, 32, AT_L2[s1] + (k * LIVE + i) * 64 + core * 32)
                        if level == 3:
                            for y in range(4):
                                piece(
                                    core * 64 + y % 2 * 32 + y // 2 * 16, 16, AT_L3[y] + (k * LIVE + i) * 32 + core * 16
                                )
                cb = pl.multiple_of(live_block(ids, level, n, role[1], i) * BLK, BLK)
                copies.append((upper.at[level, n, 0, :, pl.ds(cb, BLK)], out.at[pl.ds(AT_U[level - 1] + i * KC, KC)]))
        copies.append((nums, out.at[pl.ds(AT_NUM, NUM)]))
        start_all(copies, sems.at[n])
    wait_for(w1, sems.at[1])
    wait_for(w0, sems.at[0])


def take(src, parts, sem):
    for a, dst, b, size in parts:
        pltpu.make_async_copy(src.at[pl.ds(a, size)], dst.at[pl.ds(b, size)], sem).start()


def deal_kernel(role, w0, w1, m1, m2, m3, lo, uo, own, sems):
    parts = [(0, lo, 0, L1), (AT_U[0], uo, 0, U)]
    for y, out in ((1, m1), (2, m2), (3, m3), (0, own)):
        at = 0
        pieces = [(AT_L3[y], L3), (AT_U[2], U), (AT_NUM, NUM)]
        if y < 2:
            pieces = [(AT_L2[y], L2), (AT_U[1], U)] + pieces
        for a, size in pieces:
            parts.append((a, out, at, size))
            at += size
    for core, src in ((0, w0), (1, w1)):
        pl.when(role[2] == core)(functools.partial(take, src, parts, sems.at[0]))
    for out in (m1, m2, m3, lo, uo, own):
        wait_for(out, sems.at[0])


def choose_kernel(role, own, m1, m2, m3, zo, xo, nums, sem):
    y = role[3]
    two = ((0, zo, 0, L2), (L2, xo, 0, U), (L2 + U + L3 + U, nums, NUM, NUM))
    three = ((L2 + U, zo, L2, L3), (L2 + U + L3, xo, U, U), (L2 + U + L3 + U, nums, 2 * NUM, NUM))
    three_m = ((0, zo, L2, L3), (L3, xo, U, U), (L3 + U, nums, 2 * NUM, NUM))
    take(own, ((L2 + U + L3 + U, nums, 0, NUM),), sem)
    for odd, src in ((0, own), (1, m1)):
        pl.when(y % 2 == odd)(functools.partial(take, src, two, sem))
    for at, src, parts in ((0, own, three), (1, m1, three), (2, m2, three_m), (3, m3, three_m)):
        pl.when(y == at)(functools.partial(take, src, parts, sem))
    for out in (zo, xo, nums):
        wait_for(out, sem)


def load_panels(role, lefts, uppers, rows, l_at, u_at, la, ua, sem):
    copies = []
    for e in range(SIDE):
        lj = pl.multiple_of((role[1] ^ ORDER[e]) * KC, KC)
        uj = pl.multiple_of((role[0] ^ ORDER[e]) * KC, KC)
        for k in range(2):
            src = lefts[e].at[pl.ds(l_at + k * rows, rows)]
            copies.append((src, la.at[:, pl.ds(lj + k * 128, 128)]))
        for i in range(LIVE):
            src = uppers[e].at[pl.ds(u_at + i * KC, KC)]
            copies.append((src, ua.at[pl.ds(uj, KC), pl.ds(i * BLK, BLK)]))
    start_all(copies, sem)


def subtract(ids, role, level, n, rows, c, out):
    for i in range(LIVE):
        rb = pl.multiple_of(live_block(ids, level, n, role[0], i) * rows, rows)
        for j in range(LIVE):
            cb = pl.multiple_of(live_block(ids, level, n, role[1], j) * BLK, BLK)
            out[pl.ds(rb, rows), pl.ds(cb, BLK)] -= c[i * rows : (i + 1) * rows, j * BLK : (j + 1) * BLK]


def run_of(t, b, rows, which):
    return t[pl.ds(pl.multiple_of(b * 2 * rows + which * rows, rows), rows)]


def split(t, keep, give, rows, which):
    for b in range(SLAB):
        keep[pl.ds(b * rows, rows)] = run_of(t, b, rows, which)
        give[pl.ds(b * rows, rows)] = run_of(t, b, rows, 1 - which)


def split_coded(t, keep, give, rows, which):
    for b in range(SLAB):
        keep[pl.ds(b * rows, rows)] = run_of(t, b, rows, which)
        encode(run_of(t, b, rows, 1 - which), give.at[pl.ds(b * rows, rows)])


def encode(x, out):
    top = jnp.max(jnp.abs(x), axis=1, keepdims=True)
    e = jnp.floor(8.0 * jnp.log2(jnp.maximum(top, 1e-25)) + 0.04) - 119.0
    width = x.shape[1]
    out[:, :width] = jnp.round(x * jnp.exp2(-0.125 * e)).astype(jnp.int32).astype(jnp.int16)
    out[:, width:] = jnp.broadcast_to(e, (x.shape[0], 128)).astype(jnp.int32).astype(jnp.int16)


def decode(q):
    width = q.shape[1] - 128
    step = jnp.exp2(0.125 * q[:, width:].astype(jnp.int32).astype(F32))
    parts = [q[:, j * 128 : (j + 1) * 128].astype(jnp.int32).astype(F32) * step for j in range(width // 128)]
    return jnp.concatenate(parts, axis=1)


def update0_kernel(ids, role, front, *refs):
    lefts, uppers, (out, la, ua, sem) = refs[:4], refs[4:8], refs[8:]
    rows = LIVE * BLK
    for n in range(NODES):
        load_panels(role, lefts, uppers, rows, n * 2 * rows, n * LIVE * KC, la.at[n], ua.at[n], sem)
    out[...] = front[...]
    wait_for(la, sem)
    wait_for(ua, sem)
    for n in range(NODES):
        c = jnp.dot(la[n], ua[n], preferred_element_type=F32)
        subtract(ids, role, 0, n, BLK, c, out)


def update1_kernel(ids, role, t0, *refs):
    lefts, uppers, (keep, give, la, ua, t, sem) = refs[:4], refs[4:8], refs[8:]
    load_panels(role, lefts, uppers, LIVE * BLK, 0, 0, la, ua, sem)
    t[...] = t0[...]
    wait_for(la, sem)
    wait_for(ua, sem)
    c = jnp.dot(la[...], ua[...], preferred_element_type=F32)
    subtract(ids, role, 1, role[2], BLK, c, t)
    split(t, keep, give, 64, role[2])


def join_kernel(role, mine, theirs, keep, give, t):
    t[...] = mine[...] + theirs[...]
    split_coded(t, keep, give, 32, role[3] % 2)


def product23_kernel(role, *refs):
    lefts, uppers, (mine, other, la2, ua2, la3, ua3, sems) = refs[:4], refs[4:8], refs[8:]
    load_panels(role, lefts, uppers, LIVE * 64, 0, 0, la2, ua2, sems.at[0])
    load_panels(role, lefts, uppers, LIVE * 32, L2, U, la3, ua3, sems.at[1])
    at = 0
    for rows, la, ua, sem in ((32, la2, ua2, sems.at[0]), (16, la3, ua3, sems.at[1])):
        wait_for(la, sem)
        wait_for(ua, sem)
        c = jnp.dot(la[...], ua[...], preferred_element_type=F32)
        for i in range(LIVE):
            a, b = (c[(2 * i + k) * rows : (2 * i + k + 1) * rows] for k in range(2))
            first = role[2] == 0
            here = pl.ds(at + i * rows, rows)
            mine[here] = jnp.where(first, a, b)
            other[here] = jnp.where(first, b, a)
        at += LIVE * rows


def subtract_both(ids, role, level, at, rows, mine, theirs, t):
    here = pl.ds(at, LIVE * rows)
    subtract(ids, role, level, role[2], rows, mine[here], t)
    subtract(ids, role, level, 1 - role[2], rows, theirs[here], t)


def update2_kernel(ids, role, a, b, mine, theirs, s, sq, keep, give, t):
    total = a[...] + decode(b[...])
    s[...] = total
    t[...] = total
    subtract_both(ids, role, 2, 0, 32, mine, theirs, t)
    split_coded(t, keep, give, 16, role[3] // 2)
    encode(total, sq)


def update3_kernel(ids, role, a, b, mine, theirs, s, sq, t, tq):
    total = a[...] + decode(b[...])
    s[...] = total
    t[...] = total
    subtract_both(ids, role, 3, LIVE * 32, 16, mine, theirs, t)
    encode(t[...], tq)
    encode(total, sq)


def last_kernel(t, r, f, fq):
    total = t[...] + decode(r[...])
    f[...] = total
    encode(total, fq)


def collect_kernel(role, s1, r1, s2, *refs):
    eighths, (out, sem) = refs[:3], refs[3:]
    for odd, srcs in ((1, (s1, r1)), (0, (s2,) + eighths)):
        rows = srcs[0].shape[0]
        parts = [(src, ((0, out, j * rows, rows),)) for j, src in enumerate(srcs)]

        @pl.when(role[3] % 2 == odd)
        def _():
            for src, where in parts:
                take(src, where, sem)
    wait_for(out, sem)


def finish_kernel(role, t0, r0, s1, r1, s2, *refs):
    e2, c12, f8, e3, c3, (out, whole, buf, codes, sems) = refs[:3], refs[3], refs[4], refs[5:8], refs[8:12], refs[12:]
    core, y = role[2], role[3]

    def put(rows, where, own, own_at, coded):
        n = SLAB * rows
        mine = pltpu.make_async_copy(own, buf.at[pl.ds(0, n)], sems.at[1])
        mine.start()
        for j, (src, at) in enumerate(coded):
            pltpu.make_async_copy(src.at[pl.ds(at, n)], codes.at[pl.ds(j * n, n)], sems.at[0]).start()
        wait_for(codes.at[pl.ds(0, len(coded) * n)], sems.at[0])
        for j, first in enumerate(where):
            for b in range(SLAB):
                whole[pl.ds(b * BLK + first, rows)] = decode(codes[pl.ds(j * n + b * rows, rows)])
        mine.wait()
        for b in range(SLAB):
            whole[pl.ds(b * BLK + own_at, rows)] = buf[pl.ds(b * rows, rows)]
        flush()

    def flush():
        c = pltpu.make_async_copy(whole, out, sems.at[2])
        c.start()
        c.wait()

    @pl.when(core == 1)
    def _():
        a = pltpu.make_async_copy(t0, whole, sems.at[0])
        b = pltpu.make_async_copy(r0, buf, sems.at[1])
        a.start()
        b.start()
        a.wait()
        b.wait()
        whole[...] += buf[...]
        flush()

    @pl.when((core == 0) & (y % 2 == 1))
    def _():
        n = SLAB * 32
        put(32, (0, 96, 64), s1, 32, [(r1, 0), (c12, 0), (c12, n)])

    def eighths(own, own_y, coded):
        ys = [y ^ own_y for y in (1, 2, 3)]
        row = lambda y: y % 2 * 32 + y // 2 * 16
        put(16, [row(y) for y in ys] + [64 + row(y) for y in [own_y] + ys], own, row(own_y), coded)

    n = SLAB * 16
    pl.when((core == 0) & (y == 2))(
        lambda: eighths(s2, 2, [(r, 0) for r in e2] + [(c12, j * n) for j in range(4)])
    )
    pl.when((core == 0) & (y == 0))(
        lambda: eighths(f8, 0, [(r, 0) for r in e3] + [(r, 0) for r in c3])
    )


def grant(mib):
    return pltpu.CompilerParams(vmem_limit_bytes=mib << 20)


def sds(*shape, dtype=BF):
    return jax.ShapeDtypeStruct(shape, dtype)


def call(kernel, specs, outs, scratch, mib, *args, out_spec=VMEM):
    return pl.pallas_call(
        kernel,
        out_shape=outs,
        in_specs=specs,
        out_specs=jax.tree.map(lambda _: out_spec, outs),
        scratch_shapes=scratch,
        compiler_params=None if mib is None else grant(mib),
        cost_estimate=pl.CostEstimate(flops=1 << 30, bytes_accessed=4 << 20, transcendentals=0),
    )(*args)


def on_device(copies, left, upper, live):
    row, col, leaf = (lax.axis_index(a) for a in AXES)
    role = jnp.stack([row, col, leaf % 2, leaf // 2 % 4]).astype(jnp.int32)
    ids0 = live[:, :, 0, :]
    front = copies[0]
    cols = front.shape[1]
    dma = pltpu.SemaphoreType.DMA
    inner = SIDE * KC

    def f32(rows, width=cols):
        return sds(rows, width, dtype=F32)

    def codes(rows):
        return sds(rows, cols + 128, dtype=jnp.int16)

    def panels(rows):
        return [pltpu.VMEM((rows, inner), BF), pltpu.VMEM((inner, LIVE * BLK), BF)]

    lp0, up0 = call(
        pack0_kernel, [SMEM, SMEM, HBM, HBM],
        (sds(NODES, 2, LIVE * BLK, 128), sds(NODES, LIVE, KC, BLK)), [dma((2,))], None,
        ids0, role, left, upper,
    )
    left, upper, lp0, up0 = lax.optimization_barrier((left, upper, lp0.reshape(-1, 128), up0.reshape(-1, 128)))
    l0, u0 = gather(lp0, up0)

    w0, w1 = call(
        pack123_kernel, [SMEM, SMEM, HBM, HBM],
        (sds(PACK, 128), sds(PACK, 128)), [pltpu.VMEM((NUM, 128), BF), dma((2,))], 56,
        ids0, role, left, upper,
    )
    w1 = send(w1, flip_leaf(1))
    m1, m2, m3, lp1, up1, own = call(
        deal_kernel, [SMEM, ANY, ANY],
        (
            sds(L2 + L3 + 2 * U + NUM, 128), sds(L3 + U + NUM, 128), sds(L3 + U + NUM, 128),
            sds(L1, 128), sds(U, 128), sds(L2 + L3 + 2 * U + NUM, 128),
        ),
        [dma((1,))], 8, role, w0, w1,
    )
    m1 = send(m1, flip_leaf(2))
    m2 = send(m2, flip_leaf(4))
    m3 = send(m3, flip_leaf(6))
    l1, u1 = gather(lp1, up1)

    t0 = call(
        update0_kernel, [SMEM, SMEM, VMEM] + [ANY] * 8, f32(front.shape[0]),
        [pltpu.VMEM((NODES, LIVE * BLK, inner), BF), pltpu.VMEM((NODES, inner, LIVE * BLK), BF), dma], 12,
        ids0, role, front, *l0, *u0,
    )
    r0 = send(t0, flip_leaf(1))

    z23, x23, nums = call(
        choose_kernel, [SMEM] + [ANY] * 4,
        (sds(L2 + L3, 128), sds(2 * U, 128), sds(3 * NUM, 128)), [dma], 4,
        role, own, m1, m2, m3,
    )
    per = NODES * SIDE * LIVE
    ids = jnp.stack([nums[j * NUM, j * per : (j + 1) * per] for j in range(3)]).astype(jnp.int32)
    ids = jnp.concatenate([ids0[:1], ids.reshape(3, NODES, SIDE * LIVE)])
    l23, u23 = gather(z23, x23)

    half = SLAB * 64
    keep, give = call(
        update1_kernel, [SMEM, SMEM, VMEM] + [ANY] * 8, (f32(half), f32(half)),
        panels(LIVE * BLK) + [pltpu.VMEM(front.shape, F32), dma], 12,
        ids, role, t0, *l1, *u1,
    )
    got = send(give, flip_leaf(1))
    keep, give = call(
        join_kernel, [SMEM, VMEM, VMEM], (f32(half // 2), codes(half // 2)),
        [pltpu.VMEM((half, cols), F32)], 8, role, keep, got,
    )
    got = send(give, flip_leaf(2))

    prods = f32(LIVE * 48, LIVE * BLK)
    mine, other = call(
        product23_kernel, [SMEM] + [ANY] * 8, (prods, prods),
        panels(LIVE * 64) + panels(LIVE * 32) + [dma((2,))], 8, role, *l23, *u23,
    )
    other = send(other, flip_leaf(1))

    s1, s1q, keep, give = call(
        update2_kernel, [SMEM, SMEM] + [VMEM] * 4,
        (f32(half // 2), codes(half // 2), f32(half // 4), codes(half // 4)),
        [pltpu.VMEM((half // 2, cols), F32)], 8, ids, role, keep, got, mine, other,
    )
    got = send(give, flip_leaf(4))
    piece = (f32(half // 4), codes(half // 4))
    s2, s2q, t3, t3q = call(
        update3_kernel, [SMEM, SMEM] + [VMEM] * 4, piece + piece, [], 8,
        ids, role, keep, got, mine, other,
    )
    r3 = send(t3q, flip_leaf(8))

    r1 = send(s1q, flip_leaf(2))
    e2 = []
    for j in (1, 2, 3):
        e2.append(send(s2q, flip_leaf(2 * j)))
    c12 = call(collect_kernel, [SMEM] + [ANY] * 6, codes(half), [dma], 4, role, s1q, r1, s2q, *e2)
    c12 = send(c12, flip_leaf(1))

    f8, f8q = call(last_kernel, [VMEM, VMEM], piece, [], 8, t3, r3)
    e3 = []
    for j in (1, 2, 3):
        e3.append(send(f8q, flip_leaf(2 * j)))
    c3 = [send(q, flip_leaf(1)) for q in [f8q] + e3]

    out = call(
        finish_kernel, [SMEM] + [ANY] * 17, f32(front.shape[0]),
        [
            pltpu.VMEM(front.shape, F32), pltpu.VMEM(front.shape, F32),
            pltpu.VMEM((7 * half // 4, cols + 128), jnp.int16), dma((3,)),
        ],
        8, role, t0, r0, s1, r1, s2, *e2, c12, f8, *e3, *c3, out_spec=ANY,
    )
    return out[None]


def solution(mesh):
    in_specs = (
        P("leaf", "row", "col"),
        P(None, None, "leaf", "row", "col"),
        P(None, None, "leaf", "row", "col"),
        P(None, None, "leaf", None),
    )
    out_specs = P("leaf", "row", "col")
    return jax.shard_map(on_device, mesh=mesh, in_specs=in_specs, out_specs=out_specs, check_vma=False)
```

```python
import functools

import jax
import jax.numpy as jnp
from jax import lax
from jax.experimental import pallas as pl
from jax.experimental.pallas import tpu as pltpu
from jax.sharding import PartitionSpec as P


AXES = ("row", "col", "leaf")
SIDE = 4
LEAF = 16
BLK = 128
LIVE = 3
SLAB = 6
NODES = 2
KC = 256
BF = jnp.bfloat16
F32 = jnp.float32
ORDER = (0, 2, 1, 3)
ANY = pl.BlockSpec(memory_space=pl.ANY)
VMEM = pl.BlockSpec(memory_space=pltpu.VMEM)
HBM = pl.BlockSpec(memory_space=pltpu.HBM)
SMEM = pl.BlockSpec(memory_space=pltpu.SMEM)

L1, L2, L3, U = 2 * LIVE * BLK, 2 * LIVE * 64, 2 * LIVE * 32, LIVE * KC
NUM = 16
AT_L2 = (L1, L1 + L2)
AT_L3 = tuple(L1 + 2 * L2 + j * L3 for j in range(4))
AT_U = tuple(L1 + 2 * L2 + 4 * L3 + j * U for j in range(3))
AT_NUM = AT_U[2] + U
PACK = AT_NUM + NUM


def send(x, move):
    pairs = []
    for r in range(SIDE):
        for c in range(SIDE):
            for p in range(LEAF):
                to = move(r, c, p)
                if to is not None:
                    flat = [(a * SIDE + b) * LEAF + d for a, b, d in ((r, c, p), to)]
                    pairs.append(tuple(flat))
    return lax.ppermute(x, AXES, pairs)


def flip_leaf(bits):
    return lambda r, c, p: (r, c, p ^ bits)


def gather(left, upper):
    lefts, uppers = [left], [upper]
    for e in ORDER[1:]:
        src, hop = (lefts[1], 1) if e == 3 else (left, e)
        lefts.append(send(src, lambda r, c, p: (r, c ^ hop, p)))
        uppers.append(send(upper, lambda r, c, p: (r ^ e, c, p)))
    return lefts, uppers


def start_all(copies, sem):
    for src, dst in copies:
        pltpu.make_async_copy(src, dst, sem).start()


def wait_for(ref, sem):
    pltpu.make_async_copy(ref, ref, sem).wait()


def live_block(ids, level, n, slab, i):
    if len(ids.shape) == 1:
        number = ids[((level - 1) * NODES + n) * SIDE * LIVE + slab * LIVE + i]
    else:
        number = ids[level, n, slab * LIVE + i]
    return number - slab * SLAB


def pack0_kernel(ids, role, left, upper, lo, uo, sems):
    for n in range(NODES):
        for i in range(LIVE):
            rb = pl.multiple_of(live_block(ids, 0, n, role[0], i) * BLK, BLK)
            cb = pl.multiple_of(live_block(ids, 0, n, role[1], i) * BLK, BLK)
            lefts = [(left.at[0, n, 0, pl.ds(rb, BLK), pl.ds(k * 128, 128)], lo.at[n, k, pl.ds(i * BLK, BLK)]) for k in range(2)]
            start_all(lefts, sems.at[0])
            start_all([(upper.at[0, n, 0, :, pl.ds(cb, BLK)], uo.at[n, i])], sems.at[1])
    wait_for(lo, sems.at[0])
    wait_for(uo, sems.at[1])


def pack123_kernel(ids, role, left, upper, w0, w1, nums, sems):
    lane = lax.broadcasted_iota(jnp.int32, (NUM, 128), 1)
    row = jnp.zeros((NUM, 128), F32)
    for level in (1, 2, 3):
        for n in range(NODES):
            for i in range(SIDE * LIVE):
                at = ((level - 1) * NODES + n) * SIDE * LIVE + i
                row = jnp.where(lane == at, ids[level, n, i].astype(F32), row)
    nums[...] = row.astype(BF)
    for n, out in ((1, w1), (0, w0)):
        copies = []
        for i in range(LIVE):
            for level in (1, 2, 3):
                rb = live_block(ids, level, n, role[0], i) * BLK
                for k in range(2):
                    half = pl.ds(k * 128, 128)

                    def piece(offset, rows, at):
                        src = left.at[level, n, 0, pl.ds(pl.multiple_of(rb + offset, rows), rows), half]
                        copies.append((src, out.at[pl.ds(at, rows)]))

                    if level == 1:
                        piece(0, BLK, (k * LIVE + i) * BLK)
                    for core in range(2):
                        if level == 2:
                            for s1 in range(2):
                                piece(core * 64 + s1 * 32, 32, AT_L2[s1] + (k * LIVE + i) * 64 + core * 32)
                        if level == 3:
                            for y in range(4):
                                piece(
                                    core * 64 + y % 2 * 32 + y // 2 * 16, 16, AT_L3[y] + (k * LIVE + i) * 32 + core * 16
                                )
                cb = pl.multiple_of(live_block(ids, level, n, role[1], i) * BLK, BLK)
                copies.append((upper.at[level, n, 0, :, pl.ds(cb, BLK)], out.at[pl.ds(AT_U[level - 1] + i * KC, KC)]))
        copies.append((nums, out.at[pl.ds(AT_NUM, NUM)]))
        start_all(copies, sems.at[n])
    wait_for(w1, sems.at[1])
    wait_for(w0, sems.at[0])


def take(src, parts, sem):
    for a, dst, b, size in parts:
        pltpu.make_async_copy(src.at[pl.ds(a, size)], dst.at[pl.ds(b, size)], sem).start()


def deal_kernel(role, w0, w1, m1, m2, m3, lo, uo, own, sems):
    parts = [(0, lo, 0, L1), (AT_U[0], uo, 0, U)]
    for y, out in ((1, m1), (2, m2), (3, m3), (0, own)):
        at = 0
        pieces = [(AT_L3[y], L3), (AT_U[2], U), (AT_NUM, NUM)]
        if y < 2:
            pieces = [(AT_L2[y], L2), (AT_U[1], U)] + pieces
        for a, size in pieces:
            parts.append((a, out, at, size))
            at += size
    for core, src in ((0, w0), (1, w1)):
        pl.when(role[2] == core)(functools.partial(take, src, parts, sems.at[0]))
    for out in (m1, m2, m3, lo, uo, own):
        wait_for(out, sems.at[0])


def choose_kernel(role, own, m1, m2, m3, zo, xo, nums, sem):
    y = role[3]
    two = ((0, zo, 0, L2), (L2, xo, 0, U), (L2 + U + L3 + U, nums, NUM, NUM))
    three = ((L2 + U, zo, L2, L3), (L2 + U + L3, xo, U, U), (L2 + U + L3 + U, nums, 2 * NUM, NUM))
    three_m = ((0, zo, L2, L3), (L3, xo, U, U), (L3 + U, nums, 2 * NUM, NUM))
    take(own, ((L2 + U + L3 + U, nums, 0, NUM),), sem)
    for odd, src in ((0, own), (1, m1)):
        pl.when(y % 2 == odd)(functools.partial(take, src, two, sem))
    for at, src, parts in ((0, own, three), (1, m1, three), (2, m2, three_m), (3, m3, three_m)):
        pl.when(y == at)(functools.partial(take, src, parts, sem))
    for out in (zo, xo, nums):
        wait_for(out, sem)


def load_panels(role, lefts, uppers, rows, l_at, u_at, la, ua, sem):
    copies = []
    for e in range(SIDE):
        lj = pl.multiple_of((role[1] ^ ORDER[e]) * KC, KC)
        uj = pl.multiple_of((role[0] ^ ORDER[e]) * KC, KC)
        for k in range(2):
            src = lefts[e].at[pl.ds(l_at + k * rows, rows)]
            copies.append((src, la.at[:, pl.ds(lj + k * 128, 128)]))
        for i in range(LIVE):
            src = uppers[e].at[pl.ds(u_at + i * KC, KC)]
            copies.append((src, ua.at[pl.ds(uj, KC), pl.ds(i * BLK, BLK)]))
    start_all(copies, sem)


def subtract(ids, role, level, n, rows, c, out):
    for i in range(LIVE):
        rb = pl.multiple_of(live_block(ids, level, n, role[0], i) * rows, rows)
        for j in range(LIVE):
            cb = pl.multiple_of(live_block(ids, level, n, role[1], j) * BLK, BLK)
            out[pl.ds(rb, rows), pl.ds(cb, BLK)] -= c[i * rows : (i + 1) * rows, j * BLK : (j + 1) * BLK]


def run_of(t, b, rows, which):
    return t[pl.ds(pl.multiple_of(b * 2 * rows + which * rows, rows), rows)]


def split(t, keep, give, rows, which):
    for b in range(SLAB):
        keep[pl.ds(b * rows, rows)] = run_of(t, b, rows, which)
        give[pl.ds(b * rows, rows)] = run_of(t, b, rows, 1 - which)


def split_coded(t, keep, give, rows, which):
    for b in range(SLAB):
        keep[pl.ds(b * rows, rows)] = run_of(t, b, rows, which)
        encode(run_of(t, b, rows, 1 - which), give.at[pl.ds(b * rows, rows)])


def encode(x, out):
    top = jnp.max(jnp.abs(x), axis=1, keepdims=True)
    e = jnp.floor(8.0 * jnp.log2(jnp.maximum(top, 1e-25)) + 0.04) - 119.0
    width = x.shape[1]
    out[:, :width] = jnp.round(x * jnp.exp2(-0.125 * e)).astype(jnp.int32).astype(jnp.int16)
    out[:, width:] = jnp.broadcast_to(e, (x.shape[0], 128)).astype(jnp.int32).astype(jnp.int16)


def decode(q):
    width = q.shape[1] - 128
    step = jnp.exp2(0.125 * q[:, width:].astype(jnp.int32).astype(F32))
    parts = [q[:, j * 128 : (j + 1) * 128].astype(jnp.int32).astype(F32) * step for j in range(width // 128)]
    return jnp.concatenate(parts, axis=1)


def update0_kernel(ids, role, front, *refs):
    lefts, uppers, (out, la, ua, sem) = refs[:4], refs[4:8], refs[8:]
    rows = LIVE * BLK
    for n in range(NODES):
        load_panels(role, lefts, uppers, rows, n * 2 * rows, n * LIVE * KC, la.at[n], ua.at[n], sem)
    out[...] = front[...]
    wait_for(la, sem)
    wait_for(ua, sem)
    for n in range(NODES):
        c = jnp.dot(la[n], ua[n], preferred_element_type=F32)
        subtract(ids, role, 0, n, BLK, c, out)


def update1_kernel(ids, role, t0, *refs):
    lefts, uppers, (keep, give, la, ua, t, sem) = refs[:4], refs[4:8], refs[8:]
    load_panels(role, lefts, uppers, LIVE * BLK, 0, 0, la, ua, sem)
    t[...] = t0[...]
    wait_for(la, sem)
    wait_for(ua, sem)
    c = jnp.dot(la[...], ua[...], preferred_element_type=F32)
    subtract(ids, role, 1, role[2], BLK, c, t)
    split(t, keep, give, 64, role[2])


def join_kernel(role, mine, theirs, keep, give, t):
    t[...] = mine[...] + theirs[...]
    split_coded(t, keep, give, 32, role[3] % 2)


def product23_kernel(role, *refs):
    lefts, uppers, (mine, other, la2, ua2, la3, ua3, sems) = refs[:4], refs[4:8], refs[8:]
    load_panels(role, lefts, uppers, LIVE * 64, 0, 0, la2, ua2, sems.at[0])
    load_panels(role, lefts, uppers, LIVE * 32, L2, U, la3, ua3, sems.at[1])
    at = 0
    for rows, la, ua, sem in ((32, la2, ua2, sems.at[0]), (16, la3, ua3, sems.at[1])):
        wait_for(la, sem)
        wait_for(ua, sem)
        c = jnp.dot(la[...], ua[...], preferred_element_type=F32)
        for i in range(LIVE):
            a, b = (c[(2 * i + k) * rows : (2 * i + k + 1) * rows] for k in range(2))
            first = role[2] == 0
            here = pl.ds(at + i * rows, rows)
            mine[here] = jnp.where(first, a, b)
            other[here] = jnp.where(first, b, a)
        at += LIVE * rows


def subtract_both(ids, role, level, at, rows, mine, theirs, t):
    here = pl.ds(at, LIVE * rows)
    subtract(ids, role, level, role[2], rows, mine[here], t)
    subtract(ids, role, level, 1 - role[2], rows, theirs[here], t)


def update2_kernel(ids, role, a, b, mine, theirs, s, sq, keep, give, t):
    total = a[...] + decode(b[...])
    s[...] = total
    t[...] = total
    subtract_both(ids, role, 2, 0, 32, mine, theirs, t)
    split_coded(t, keep, give, 16, role[3] // 2)
    encode(total, sq)


def update3_kernel(ids, role, a, b, mine, theirs, s, sq, t, tq):
    total = a[...] + decode(b[...])
    s[...] = total
    t[...] = total
    subtract_both(ids, role, 3, LIVE * 32, 16, mine, theirs, t)
    encode(t[...], tq)
    encode(total, sq)


def last_kernel(t, r, f, fq):
    total = t[...] + decode(r[...])
    f[...] = total
    encode(total, fq)


def collect_kernel(role, s1, r1, s2, *refs):
    eighths, (out, sem) = refs[:3], refs[3:]
    for odd, srcs in ((1, (s1, r1)), (0, (s2,) + eighths)):
        rows = srcs[0].shape[0]
        parts = [(src, ((0, out, j * rows, rows),)) for j, src in enumerate(srcs)]

        @pl.when(role[3] % 2 == odd)
        def _():
            for src, where in parts:
                take(src, where, sem)
    wait_for(out, sem)


def finish_kernel(role, t0, r0, s1, r1, s2, *refs):
    e2, c12, f8, e3, c3, (out, whole, buf, codes, sems) = refs[:3], refs[3], refs[4], refs[5:8], refs[8:12], refs[12:]
    core, y = role[2], role[3]

    def put(rows, where, own, own_at, coded):
        n = SLAB * rows
        mine = pltpu.make_async_copy(own, buf.at[pl.ds(0, n)], sems.at[1])
        mine.start()
        for j, (src, at) in enumerate(coded):
            pltpu.make_async_copy(src.at[pl.ds(at, n)], codes.at[pl.ds(j * n, n)], sems.at[0]).start()
        wait_for(codes.at[pl.ds(0, len(coded) * n)], sems.at[0])
        for j, first in enumerate(where):
            for b in range(SLAB):
                whole[pl.ds(b * BLK + first, rows)] = decode(codes[pl.ds(j * n + b * rows, rows)])
        mine.wait()
        for b in range(SLAB):
            whole[pl.ds(b * BLK + own_at, rows)] = buf[pl.ds(b * rows, rows)]
        flush()

    def flush():
        c = pltpu.make_async_copy(whole, out, sems.at[2])
        c.start()
        c.wait()

    @pl.when(core == 1)
    def _():
        a = pltpu.make_async_copy(t0, whole, sems.at[0])
        b = pltpu.make_async_copy(r0, buf, sems.at[1])
        a.start()
        b.start()
        a.wait()
        b.wait()
        whole[...] += buf[...]
        flush()

    @pl.when((core == 0) & (y % 2 == 1))
    def _():
        n = SLAB * 32
        put(32, (0, 96, 64), s1, 32, [(r1, 0), (c12, 0), (c12, n)])

    def eighths(own, own_y, coded):
        ys = [y ^ own_y for y in (1, 2, 3)]
        row = lambda y: y % 2 * 32 + y // 2 * 16
        put(16, [row(y) for y in ys] + [64 + row(y) for y in [own_y] + ys], own, row(own_y), coded)

    n = SLAB * 16
    pl.when((core == 0) & (y == 2))(
        lambda: eighths(s2, 2, [(r, 0) for r in e2] + [(c12, j * n) for j in range(4)])
    )
    pl.when((core == 0) & (y == 0))(
        lambda: eighths(f8, 0, [(r, 0) for r in e3] + [(r, 0) for r in c3])
    )


def grant(mib):
    return pltpu.CompilerParams(vmem_limit_bytes=mib << 20)


def sds(*shape, dtype=BF):
    return jax.ShapeDtypeStruct(shape, dtype)


def call(kernel, specs, outs, scratch, mib, *args, out_spec=VMEM):
    return pl.pallas_call(
        kernel,
        out_shape=outs,
        in_specs=specs,
        out_specs=jax.tree.map(lambda _: out_spec, outs),
        scratch_shapes=scratch,
        compiler_params=None if mib is None else grant(mib),
        cost_estimate=pl.CostEstimate(flops=1 << 30, bytes_accessed=4 << 20, transcendentals=0),
    )(*args)


def on_device(copies, left, upper, live):
    row, col, leaf = (lax.axis_index(a) for a in AXES)
    role = jnp.stack([row, col, leaf % 2, leaf // 2 % 4]).astype(jnp.int32)
    ids0 = live[:, :, 0, :]
    front = copies[0]
    cols = front.shape[1]
    dma = pltpu.SemaphoreType.DMA
    inner = SIDE * KC

    def f32(rows, width=cols):
        return sds(rows, width, dtype=F32)

    def codes(rows):
        return sds(rows, cols + 128, dtype=jnp.int16)

    def panels(rows):
        return [pltpu.VMEM((rows, inner), BF), pltpu.VMEM((inner, LIVE * BLK), BF)]

    lp0, up0 = call(
        pack0_kernel, [SMEM, SMEM, HBM, HBM],
        (sds(NODES, 2, LIVE * BLK, 128), sds(NODES, LIVE, KC, BLK)), [dma((2,))], None,
        ids0, role, left, upper,
    )
    left, upper, lp0, up0 = lax.optimization_barrier((left, upper, lp0.reshape(-1, 128), up0.reshape(-1, 128)))
    l0, u0 = gather(lp0, up0)

    w0, w1 = call(
        pack123_kernel, [SMEM, SMEM, HBM, HBM],
        (sds(PACK, 128), sds(PACK, 128)), [pltpu.VMEM((NUM, 128), BF), dma((2,))], 56,
        ids0, role, left, upper,
    )
    w1 = send(w1, flip_leaf(1))
    m1, m2, m3, lp1, up1, own = call(
        deal_kernel, [SMEM, ANY, ANY],
        (
            sds(L2 + L3 + 2 * U + NUM, 128), sds(L3 + U + NUM, 128), sds(L3 + U + NUM, 128),
            sds(L1, 128), sds(U, 128), sds(L2 + L3 + 2 * U + NUM, 128),
        ),
        [dma((1,))], 8, role, w0, w1,
    )
    m1 = send(m1, flip_leaf(2))
    m2 = send(m2, flip_leaf(4))
    m3 = send(m3, flip_leaf(6))
    l1, u1 = gather(lp1, up1)

    t0 = call(
        update0_kernel, [SMEM, SMEM, VMEM] + [ANY] * 8, f32(front.shape[0]),
        [pltpu.VMEM((NODES, LIVE * BLK, inner), BF), pltpu.VMEM((NODES, inner, LIVE * BLK), BF), dma], 12,
        ids0, role, front, *l0, *u0,
    )
    r0 = send(t0, flip_leaf(1))

    z23, x23, nums = call(
        choose_kernel, [SMEM] + [ANY] * 4,
        (sds(L2 + L3, 128), sds(2 * U, 128), sds(3 * NUM, 128)), [dma], 4,
        role, own, m1, m2, m3,
    )
    lane = jnp.arange(128, dtype=jnp.int32) // (NODES * SIDE * LIVE)
    ids = sum(jnp.where(lane == j, nums[j * NUM], 0) for j in range(3)).astype(jnp.int32)
    l23, u23 = gather(z23, x23)

    half = SLAB * 64
    keep, give = call(
        update1_kernel, [SMEM, SMEM, VMEM] + [ANY] * 8, (f32(half), f32(half)),
        panels(LIVE * BLK) + [pltpu.VMEM(front.shape, F32), dma], 12,
        ids, role, t0, *l1, *u1,
    )
    got = send(give, flip_leaf(1))
    keep, give = call(
        join_kernel, [SMEM, VMEM, VMEM], (f32(half // 2), codes(half // 2)),
        [pltpu.VMEM((half, cols), F32)], 8, role, keep, got,
    )
    got = send(give, flip_leaf(2))

    prods = f32(LIVE * 48, LIVE * BLK)
    mine, other = call(
        product23_kernel, [SMEM] + [ANY] * 8, (prods, prods),
        panels(LIVE * 64) + panels(LIVE * 32) + [dma((2,))], 8, role, *l23, *u23,
    )
    other = send(other, flip_leaf(1))

    s1, s1q, keep, give = call(
        update2_kernel, [SMEM, SMEM] + [VMEM] * 4,
        (f32(half // 2), codes(half // 2), f32(half // 4), codes(half // 4)),
        [pltpu.VMEM((half // 2, cols), F32)], 8, ids, role, keep, got, mine, other,
    )
    got = send(give, flip_leaf(4))
    piece = (f32(half // 4), codes(half // 4))
    s2, s2q, t3, t3q = call(
        update3_kernel, [SMEM, SMEM] + [VMEM] * 4, piece + piece, [], 8,
        ids, role, keep, got, mine, other,
    )
    r3 = send(t3q, flip_leaf(8))

    r1 = send(s1q, flip_leaf(2))
    e2 = []
    for j in (1, 2, 3):
        e2.append(send(s2q, flip_leaf(2 * j)))
    c12 = call(collect_kernel, [SMEM] + [ANY] * 6, codes(half), [dma], 4, role, s1q, r1, s2q, *e2)
    c12 = send(c12, flip_leaf(1))

    f8, f8q = call(last_kernel, [VMEM, VMEM], piece, [], 8, t3, r3)
    e3 = []
    for j in (1, 2, 3):
        e3.append(send(f8q, flip_leaf(2 * j)))
    c3 = [send(q, flip_leaf(1)) for q in [f8q] + e3]

    out = call(
        finish_kernel, [SMEM] + [ANY] * 17, f32(front.shape[0]),
        [
            pltpu.VMEM(front.shape, F32), pltpu.VMEM(front.shape, F32),
            pltpu.VMEM((7 * half // 4, cols + 128), jnp.int16), dma((3,)),
        ],
        8, role, t0, r0, s1, r1, s2, *e2, c12, f8, *e3, *c3, out_spec=ANY,
    )
    return out[None]


def solution(mesh):
    in_specs = (
        P("leaf", "row", "col"),
        P(None, None, "leaf", "row", "col"),
        P(None, None, "leaf", "row", "col"),
        P(None, None, "leaf", None),
    )
    out_specs = P("leaf", "row", "col")
    return jax.shard_map(on_device, mesh=mesh, in_specs=in_specs, out_specs=out_specs, check_vma=False)
```
